32 devices in a mesh: groups: 2 (over x), month: 16 (over z, y, core).
Axes of the slice: x: 2, y: 2, z: 4, core: 2. Of those that a mesh axis runs over, the one named last changes fastest.
Arguments:
- shocks: float32 [512, 4096], P('month', 'groups'), parts along dimension 1, may hold values from -6 to 6
- long_mean: float32 [512], P('month'), may hold values from 0 to 0.08
- reversion: float32 [4096], P('groups'), parts along dimension 0, may hold values from 0.1 to 1
- volatility: float32 [4096], P('groups'), parts along dimension 0, may hold values from 0.004 to 0.015
- start_rate: float32 [4096], P('groups'), parts along dimension 0, may hold values from 0 to 0.06
- cash_flows: bfloat16 [3, 512, 24576], P(None, 'month', 'groups'), parts along dimension 2, may hold values from -0.5 to 0.5
Outputs:
- present: bfloat16 [3, 24576, 2048], P(None, ('groups', 'month')), parts along dimension 1
The draws below stay inside these ranges and needn't reach their ends.
There are 2 independent parts, one for each index of `groups`. The reference program is written for one: setup_inputs(seed, part) draws one part's arguments, and reference() takes and returns one part's arrays. A program takes and returns all parts, laid end to end along the dimension named above; an argument that names none is the same for every part. Nothing has to cross between parts.
All inputs are finite; a program needn't handle non-finite values.
Results may differ from the reference program's by a relative error of at most 0.0049.
Values may be sent and summed in bfloat16 or wider, within the bound.
A program may use at most 192 MiB of HBM per device.

```python
import math
import jax
import jax.numpy as jnp
from jax import lax

LEGS = 3
MONTHS = 512
SCENARIOS = 2048
CELLS = 12288


def block_scale(own_key, dims, pieces, least, high):
    def one(dim, blocks):
        steps = jax.random.uniform(jax.random.fold_in(jax.random.fold_in(own_key, 6), dim), (blocks,), jnp.float32, least / len(pieces), high / len(pieces))
        return jnp.repeat(jnp.exp(steps), dims[dim] // blocks).reshape((-1,) + (1,) * (len(dims) - dim - 1))

    level = one(*pieces[0])
    for cut in pieces[1:]:
        level = level * one(*cut)
    return level


def gaussian(key, extent, deviation, bound, pieces=(), dtype=jnp.bfloat16):
    drawn = deviation * jax.random.normal(key, extent, jnp.float32)
    if pieces:
        drawn = drawn * block_scale(key, extent, pieces, -0.22, 0.18)
    return jnp.clip(drawn, -bound, bound).astype(dtype)


def setup_inputs(seed: int = 0, part: int = 0) -> dict:
    seeds = jax.random.split(jax.random.key(seed), 7)
    part_keys = jax.random.split(jax.random.fold_in(seeds[6], part), 7)
    shocks = gaussian(part_keys[0], (MONTHS, SCENARIOS), 1.0, 6.0, ((0, 16),), jnp.float32)
    long_mean = jnp.clip(0.08 * jax.random.uniform(seeds[1], (MONTHS,), jnp.float32) ** block_scale(seeds[1], (MONTHS,), ((0, 16),), -0.2, 0.2), 0.0, 0.08)
    reversion = jnp.clip(jnp.exp(jax.random.uniform(part_keys[2], (SCENARIOS,), jnp.float32, math.log(0.1), math.log(1.0))), 0.1, 1.0)
    volatility = jnp.clip(jnp.exp(jax.random.uniform(part_keys[3], (SCENARIOS,), jnp.float32, math.log(0.004), math.log(0.015))), 0.004, 0.015)
    start_rate = jnp.clip(jax.random.uniform(part_keys[4], (SCENARIOS,), jnp.float32, 0.0, 0.06), 0.0, 0.06)
    cash_flows = gaussian(part_keys[5], (LEGS, MONTHS, CELLS), (MONTHS // 4) ** -0.5, 0.5, ((1, 16),))
    return dict(shocks=shocks, long_mean=long_mean, reversion=reversion, volatility=volatility, start_rate=start_rate, cash_flows=cash_flows)


month_step = 1.0 / 12.0
root_step = math.sqrt(1.0 / 12.0)
risk_price = 0.15
price_scale = risk_price * math.sqrt(12.0)
price_drift = 0.5 * risk_price * risk_price

def reference(shocks, long_mean, reversion, volatility, start_rate, cash_flows):
    persist = 1.0 - reversion * month_step

    def advance(carry, inputs):
        rate, total = carry
        shock_row, level = inputs
        drive = reversion * month_step * level + volatility * root_step * shock_row
        rate = persist * rate + drive
        total = total + rate + price_scale * shock_row + price_drift
        return ((rate, total), jnp.exp(-month_step * total).astype(jnp.bfloat16))
    initial = (start_rate, jnp.zeros_like(start_rate))
    final_state, discount = lax.scan(advance, initial, (shocks, long_mean))
    blocks = []
    for leg_index in range(cash_flows.shape[0]):
        value = lax.dot_general(cash_flows[leg_index], discount, (((0,), (0,)), ((), ())), preferred_element_type=jnp.float32)
        blocks.append(value.astype(jnp.bfloat16))
    return jnp.stack(blocks)
```

```python
import functools
import math

import jax
import jax.numpy as jnp
from jax import lax
from jax.experimental import pallas as pl
from jax.experimental.pallas import tpu as pltpu
from jax.sharding import PartitionSpec as P

month_step = 1.0 / 12.0
root_step = math.sqrt(1.0 / 12.0)
risk_price = 0.15
price_scale = risk_price * math.sqrt(12.0)
price_drift = 0.5 * risk_price * risk_price
MESH = pl.DeviceIdType.MESH
CORES = 2
VMEM_BYTES = 67_043_328
SLACK = 65536


WINDOW, EARLY, PARTS, LEVELS, OWN, LAST = 8, 4, 10, 12, 14, 4
PIECES, SIDE_PIECES = 1, 1


def partners(n, me, step):
    if n & (n - 1):
        return (me + step) % n, (me + n - step) % n
    other, bit = me, 1
    while bit < n:
        if step & bit:
            other = other + bit * (1 - 2 * (me // bit % 2))
        bit *= 2
    return other, other


def weave(far, near):
    total = len(far) + len(near)
    out, taken = [], 0
    for i in range(total):
        if taken * total < (i + 1) * len(far) and taken < len(far):
            out.append(far[taken])
            taken += 1
        else:
            out.append(near[i - taken])
    return out


def orders(n, team, legs):
    far = [k for k in range(n // 2, n)]
    near = [k for k in range(team, n // 2)]
    home = [k for k in range(1, min(team, n))]
    low = [(leg, k) for leg in range(legs) for k in home]
    low, rest = low[:EARLY], low[EARLY:]
    high = []
    for leg in range(legs):
        close = [(leg, k) for k in near] + [k for k in rest if k[0] == leg]
        low += weave([(leg, k) for k in far], close)
        high += [(leg, k) for k in weave(far, home + near)]
    return low, high


def product(flows, discount, first, cells, out, row, after=None):
    width = discount.shape[1]
    tall, wide = math.gcd(cells, 256), math.gcd(width, 1024)
    for tile in range(cells // tall):
        for c in range(width // wide):
            cols = pl.ds(c * wide, wide)
            value = lax.dot_general(
                flows[:, pl.ds(first + tile * tall, tall)],
                discount[:, cols],
                (((0,), (0,)), ((), ())),
                preferred_element_type=jnp.float32,
            )
            out[pl.ds(row + tile * tall, tall), cols] = value.astype(jnp.bfloat16)
        if after is not None:
            after(tile, tall)


def finish(flows, discount, done, out, last, sems):
    cells = last.shape[0]
    ready, width = done.shape
    parts = ready // cells

    def ship(k):
        rows = pl.ds(k * cells, cells)
        return pltpu.make_async_copy(done.at[rows], out.at[rows], sems.at[k])

    def tail(tile, tall):
        return pltpu.make_async_copy(
            last.at[pl.ds(tile * tall, tall)],
            out.at[pl.ds(ready + tile * tall, tall)],
            sems.at[parts + tile],
        )

    for k in range(parts):
        ship(k).start()
    product(flows, discount, ready, cells, last, 0, lambda tile, tall: tail(tile, tall).start())
    for k in range(parts):
        ship(k).wait()
    tall = math.gcd(cells, 256)
    for tile in range(cells // tall):
        tail(tile, tall).wait()


def kernel(
    n,
    sides,
    shocks,
    long_mean,
    reversion,
    volatility,
    start_rate,
    cash_flows,
    flows_out,
    discount_out,
    done_out,
    reach_ref,
    total_ref,
    part_ref,
    level_ref,
    flow_send,
    flow_recv,
    part_send,
    part_recv,
    level_send,
    level_recv,
    up_send,
    up_recv,
    down_send,
    down_recv,
    side_send,
    side_recv,
    twin_send,
    twin_recv,
    own_sem,
    ready,
):
    rows, width = shocks.shape
    legs = cash_flows.shape[0]
    own = cash_flows.shape[2] // n
    team = sides * CORES
    depth = n // team
    me = lax.axis_index("month")
    z, spot = me // team, me % team
    side, core = spot // CORES, spot % CORES
    place = lambda z, side, core: (z * sides + side) * CORES + core

    def remote(src, dst, send, recv, device):
        return pltpu.make_async_remote_copy(
            src_ref=src,
            dst_ref=dst,
            send_sem=send,
            recv_sem=recv,
            device_id={"month": device},
            device_id_type=MESH,
        )

    barrier = pltpu.get_barrier_semaphore()

    def greet(semaphore, device):
        pl.semaphore_signal(semaphore, inc=1, device_id={"month": device}, device_id_type=MESH)

    for k in range(1, team):
        greet(barrier, z * team + (spot + k) % team)
    for k in range(1, depth):

        @pl.when(z + k < depth)
        def _():
            for j in range(team):
                greet(barrier, (z + k) * team + j)

    def keep(leg):
        return pltpu.make_async_copy(
            cash_flows.at[leg, :, pl.ds(pl.multiple_of(me * own, own), own)],
            flows_out.at[pl.ds(pl.multiple_of(me * rows, rows), rows), pl.ds(leg * own, own)],
            own_sem.at[leg],
        )

    for leg in range(legs):
        keep(leg).start()
    pl.semaphore_wait(barrier, z * team + team - 1)
    for k in range(1, depth):

        @pl.when(z - k >= 0)
        def _():
            for j in range(team):
                greet(ready.at[z], (z - k) * team + j)

    upper = z * 2 // depth
    low_order, high_order = orders(n, team, legs)

    def flow_copy(leg, slot, sender, receiver, device):
        return remote(
            cash_flows.at[leg, :, pl.ds(pl.multiple_of(receiver * own, own), own)],
            flows_out.at[pl.ds(pl.multiple_of(sender * rows, rows), rows), pl.ds(leg * own, own)],
            flow_send.at[slot],
            flow_recv.at[slot],
            device,
        )

    def flow_out(i):
        (leg_a, step_a), (leg_b, step_b) = low_order[i], high_order[i]
        leg = leg_a + upper * (leg_b - leg_a)
        step = step_a + upper * (step_b - step_a)
        to_a, to_b = partners(n, me, step_a)[0], partners(n, me, step_b)[0]
        to = to_a + upper * (to_b - to_a)
        return flow_copy(leg, leg * (n - 1) + step - 1, me, to, to)

    def flow_in(leg, step):
        source = partners(n, me, step)[1]
        return flow_copy(leg, leg * (n - 1) + step - 1, source, me, source)

    count = (n - 1) * legs
    started, sent = [0], [0]

    def fill(upto, window=WINDOW):
        for i in range(started[0], min(count, upto)):
            while i - sent[0] >= window:
                flow_out(sent[0]).wait_send()
                sent[0] += 1
            flow_out(i).start()
            started[0] += 1

    fill(EARLY)

    chunk = math.gcd(width, 512)
    unit = jnp.ones((1, chunk), jnp.float32)
    zero = jnp.zeros((1, chunk), jnp.float32)
    last = []
    for c in range(width // chunk):
        lanes = pl.ds(c * chunk, chunk)
        pull = reversion[lanes].reshape(1, chunk) * month_step
        sway = volatility[lanes].reshape(1, chunk) * root_step
        persist = 1.0 - pull

        def month(t, carry):
            rate, power, reach, total = carry
            shock = shocks[pl.ds(t, 1), lanes]
            rate = persist * rate + (pull * long_mean[t] + sway * shock)
            power = persist * power
            reach = reach + power
            total = total + (rate + price_scale * shock + price_drift)
            reach_ref[pl.ds(t, 1), lanes] = reach
            total_ref[pl.ds(t, 1), lanes] = total
            return rate, power, reach, total

        rate, power, reach, total = lax.fori_loop(
            0, rows, month, (zero, unit, zero, zero), unroll=4
        )
        part_ref[spot, 0:1, lanes] = rate
        part_ref[spot, 1:2, lanes] = total
        last.append((power, reach))
    power = jnp.concatenate([one[0] for one in last], axis=1)
    reach = jnp.concatenate([one[1] for one in last], axis=1)

    def part_copy(k, slot, device):
        return remote(
            part_ref.at[slot], part_ref.at[slot], part_send.at[k], part_recv.at[k], device
        )

    for k in range(1, team):
        part_copy(k, spot, z * team + (spot + k) % team).start()
    for k in range(1, depth):

        @pl.when(z + k < depth)
        def _():
            pl.semaphore_wait(ready.at[z + k], team)

    fill(PARTS)
    for k in range(1, team):
        source = (spot + team - k) % team
        part_copy(k, source, z * team + source).wait_recv()

    rate, total = part_ref[0, 0:1], part_ref[0, 1:2]
    level_power, level_reach = power, reach
    for j in range(1, team):
        rate, total = (
            power * rate + part_ref[j, 0:1],
            total + reach * rate + part_ref[j, 1:2],
        )
        level_reach = level_reach + reach * level_power
        level_power = power * level_power
    level_ref[z, 0:1] = rate
    level_ref[z, 1:2] = total

    def level_copy(k, slot, device):
        return remote(
            level_ref.at[slot], level_ref.at[slot], level_send.at[k], level_recv.at[k], device
        )

    for k in range(1, depth):

        @pl.when(z + k < depth)
        def _():
            level_copy(k, z, place(z + k, side, core)).start()

    fill(LEVELS)

    for k in range(1, depth):

        @pl.when(z - k >= 0)
        def _():
            level_copy(k, z - k, place(z - k, side, core)).wait_recv()

    def past_level(j, state):
        rate, total = state
        return (
            level_power * rate + level_ref[j, 0:1],
            total + level_reach * rate + level_ref[j, 1:2],
        )

    def past_part(j, state):
        rate, total = state
        return power * rate + part_ref[j, 0:1], total + reach * rate + part_ref[j, 1:2]

    state = (start_rate[...].reshape(1, width), jnp.zeros((1, width), jnp.float32))
    state = lax.fori_loop(0, z, past_level, state)
    rate, total = lax.fori_loop(0, spot, past_part, state)
    exponent = total + reach_ref[...] * rate + total_ref[...]
    discount_out[pl.ds(pl.multiple_of(me * rows, rows), rows), :] = jnp.exp(
        -month_step * exponent
    ).astype(jnp.bfloat16)

    def months(m, lanes=slice(None)):
        return discount_out.at[pl.ds(pl.multiple_of(m * rows, rows), rows), lanes]

    waits = []

    def send(cond, make, pieces=1):
        waits.append((cond, make))

        def go():
            for k in range(pieces):
                make(pl.ds(k * (width // pieces), width // pieces)).start()

        if cond is None:
            go()
        else:
            pl.when(cond)(go)

    def shard_copy(shard, lanes, send_sem, recv_sem, device):
        ref = months(shard) if lanes is None else months(shard, lanes)
        return remote(ref, ref, send_sem, recv_sem, device)

    def up_copy(h, shard, device, lanes=None):
        return shard_copy(shard, lanes, up_send.at[h], up_recv.at[h], device)

    def down_copy(h, shard, device, lanes=None):
        return shard_copy(shard, lanes, down_send.at[h], down_recv.at[h], device)

    def side_copy(level, shard, device, lanes=None):
        return shard_copy(shard, lanes, side_send.at[level], side_recv.at[level], device)

    def twin_copy(level, lane, shard, device, lanes=None):
        slot = level * sides + lane
        return shard_copy(shard, lanes, twin_send.at[slot], twin_recv.at[slot], device)

    def beside(cond, level):
        shard = place(level, side, core)
        if sides > 1:
            send(
                cond,
                lambda lanes=None: side_copy(level, shard, place(z, 1 - side, core), lanes),
                SIDE_PIECES,
            )
        send(cond, lambda lanes=None: twin_copy(level, side, shard, place(z, side, 1 - core), lanes))

    def across(cond, level):
        shard = place(level, 1 - side, core)

        def take():
            side_copy(level, shard, place(z, 1 - side, core)).wait_recv()

        if cond is None:
            take()
        else:
            pl.when(cond)(take)
        send(
            cond,
            lambda lanes=None: twin_copy(level, 1 - side, shard, place(z, side, 1 - core), lanes),
        )

    def rise(cond, h, shard):
        send(
            cond,
            lambda lanes=None: up_copy(h, shard, place(z + 1, side, core), lanes),
            PIECES,
        )

    def sink(cond, h, shard):
        send(
            cond,
            lambda lanes=None: down_copy(h, shard, place(z - 1, side, core), lanes),
            PIECES,
        )

    rise(z + 1 < depth, 0, me)
    sink(z > 0, 0, me)
    beside(None, z)
    pace = (count - OWN - LAST) // depth
    fill(OWN + pace)
    for h in range(1, depth):
        low, high = place(z - h, side, core), place(z + h, side, core)

        @pl.when(z - h >= 0)
        def _():
            up_copy(h - 1, low, place(z - 1, side, core)).wait_recv()

        rise((z - h >= 0) & (z + 1 < depth), h, low)

        @pl.when(z + h < depth)
        def _():
            down_copy(h - 1, high, place(z + 1, side, core)).wait_recv()

        sink((z + h < depth) & (z > 0), h, high)
        beside(z - h >= 0, z - h)
        beside(z + h < depth, z + h)
        if sides > 1:
            if h == 1:
                across(None, z)
            else:
                across(z - h + 1 >= 0, z - h + 1)
                across(z + h - 1 < depth, z + h - 1)
        fill(OWN + (1 + h) * pace)
    if sides > 1:
        if depth == 1:
            across(None, z)
        else:
            across(z - depth + 1 >= 0, z - depth + 1)
            across(z + depth - 1 < depth, z + depth - 1)
    fill(count, count)

    for level in range(depth):
        for lane in range(sides):
            shard = place(level, lane, 1 - core)
            twin_copy(level, lane, shard, place(z, side, 1 - core)).wait_recv()
    for leg in range(legs):
        for step in range(1, n):
            flow_in(leg, step).wait_recv()
        keep(leg).wait()
        if leg < legs - 1:
            product(flows_out, discount_out, leg * own, own, done_out, leg * own)
    for k in range(1, team):
        part_copy(k, spot, z * team + (spot + k) % team).wait_send()
    for k in range(1, depth):

        @pl.when(z + k < depth)
        def _():
            level_copy(k, z, place(z + k, side, core)).wait_send()

    for cond, make in waits:
        if cond is None:
            make().wait_send()
        else:
            pl.when(cond)(lambda make=make: make().wait_send())
    for i in range(sent[0], count):
        flow_out(i).wait_send()


def local(n, sides, shocks, long_mean, reversion, volatility, start_rate, cash_flows):
    rows, width = shocks.shape
    legs, _, cells = cash_flows.shape
    own = cells // n
    team = sides * CORES
    depth = n // team
    count = (n - 1) * legs
    held = 2 * (n * rows * (legs * own + width) + (legs - 1) * own * width) + SLACK
    dma = pltpu.SemaphoreType.DMA
    vmem = pl.BlockSpec(memory_space=pltpu.VMEM)
    anywhere = pl.BlockSpec(memory_space=pltpu.HBM)
    flows, discount, done = pl.pallas_call(
        functools.partial(kernel, n, sides),
        out_shape=(
            pltpu.VMEM((n * rows, legs * own), jnp.bfloat16),
            pltpu.VMEM((n * rows, width), jnp.bfloat16),
            pltpu.VMEM(((legs - 1) * own, width), jnp.bfloat16),
        ),
        in_specs=[vmem, pl.BlockSpec(memory_space=pltpu.SMEM), vmem, vmem, vmem, anywhere],
        out_specs=(vmem, vmem, vmem),
        scratch_shapes=[
            pltpu.VMEM((rows, width), jnp.float32),
            pltpu.VMEM((rows, width), jnp.float32),
            pltpu.VMEM((team, 2, width), jnp.float32),
            pltpu.VMEM((depth, 2, width), jnp.float32),
            dma((count,)),
            dma((count,)),
            dma((team,)),
            dma((team,)),
            dma((depth,)),
            dma((depth,)),
            dma((depth,)),
            dma((depth,)),
            dma((depth,)),
            dma((depth,)),
            dma((depth,)),
            dma((depth,)),
            dma((n // CORES,)),
            dma((n // CORES,)),
            dma((legs,)),
            pltpu.SemaphoreType.REGULAR((depth,)),
        ],
        compiler_params=pltpu.CompilerParams(
            collective_id=0, has_side_effects=True, vmem_limit_bytes=VMEM_BYTES - held
        ),
        name="exchange",
    )(shocks, long_mean, reversion, volatility, start_rate, cash_flows)
    tiles = own // math.gcd(own, 256)
    present = pl.pallas_call(
        finish,
        out_shape=jax.ShapeDtypeStruct((legs * own, width), jnp.bfloat16),
        in_specs=[vmem, vmem, vmem],
        out_specs=anywhere,
        scratch_shapes=[
            pltpu.VMEM((own, width), jnp.bfloat16),
            dma((legs - 1 + tiles,)),
        ],
        compiler_params=pltpu.CompilerParams(vmem_limit_bytes=16 << 20),
        name="finish",
    )(flows, discount, done)
    return present.reshape(legs, own, width)


def solution(mesh):
    n = mesh.shape["month"]
    sides = max(1, 4 // mesh.shape["groups"])
    placed = (
        P("month", "groups"),
        P("month"),
        P("groups"),
        P("groups"),
        P("groups"),
        P(None, "month", "groups"),
    )
    return jax.shard_map(
        functools.partial(local, n, sides),
        mesh=mesh,
        in_specs=placed,
        out_specs=P(None, ("groups", "month"), None),
        check_vma=False,
    )
```

```python
import functools
import math

import jax
import jax.numpy as jnp
from jax import lax
from jax.experimental import pallas as pl
from jax.experimental.pallas import tpu as pltpu
from jax.sharding import PartitionSpec as P

month_step = 1.0 / 12.0
root_step = math.sqrt(1.0 / 12.0)
risk_price = 0.15
price_scale = risk_price * math.sqrt(12.0)
price_drift = 0.5 * risk_price * risk_price
MESH = pl.DeviceIdType.MESH
CORES = 2
VMEM_BYTES = 67_043_328
SLACK = 65536


WINDOW, EARLY, PARTS, LEVELS, OWN, LAST = 8, 4, 10, 12, 14, 4
PIECES, SIDE_PIECES = 1, 1


def partners(n, me, step):
    if n & (n - 1):
        return (me + step) % n, (me + n - step) % n
    other, bit = me, 1
    while bit < n:
        if step & bit:
            other = other + bit * (1 - 2 * (me // bit % 2))
        bit *= 2
    return other, other


def weave(far, near):
    total = len(far) + len(near)
    out, taken = [], 0
    for i in range(total):
        if taken * total < (i + 1) * len(far) and taken < len(far):
            out.append(far[taken])
            taken += 1
        else:
            out.append(near[i - taken])
    return out


def orders(n, team, legs):
    far = [k for k in range(n // 2, n)]
    near = [k for k in range(team, n // 2)]
    home = [k for k in range(1, min(team, n))]
    low = [(leg, k) for leg in range(legs) for k in home]
    low, rest = low[:EARLY], low[EARLY:]
    high = []
    for leg in range(legs):
        close = [(leg, k) for k in near] + [k for k in rest if k[0] == leg]
        low += weave([(leg, k) for k in far], close)
        high += [(leg, k) for k in weave(far, home + near)]
    return low, high


def product(flows, discount, first, cells, out, row, after=None):
    width = discount.shape[1]
    tall, wide = math.gcd(cells, 256), math.gcd(width, 1024)
    for tile in range(cells // tall):
        for c in range(width // wide):
            cols = pl.ds(c * wide, wide)
            value = lax.dot_general(
                flows[:, pl.ds(first + tile * tall, tall)],
                discount[:, cols],
                (((0,), (0,)), ((), ())),
                preferred_element_type=jnp.float32,
            )
            out[pl.ds(row + tile * tall, tall), cols] = value.astype(jnp.bfloat16)
        if after is not None:
            after(tile, tall)


def finish(flows, discount, done, out, last, sems):
    cells = last.shape[0]
    ready, width = done.shape
    parts = ready // cells

    def ship(k):
        rows = pl.ds(k * cells, cells)
        return pltpu.make_async_copy(done.at[rows], out.at[rows], sems.at[k])

    def tail(tile, tall):
        return pltpu.make_async_copy(
            last.at[pl.ds(tile * tall, tall)],
            out.at[pl.ds(ready + tile * tall, tall)],
            sems.at[parts + tile],
        )

    for k in range(parts):
        ship(k).start()
    product(flows, discount, ready, cells, last, 0, lambda tile, tall: tail(tile, tall).start())
    for k in range(parts):
        ship(k).wait()
    tall = math.gcd(cells, 256)
    for tile in range(cells // tall):
        tail(tile, tall).wait()


def kernel(
    n,
    sides,
    shocks,
    long_mean,
    reversion,
    volatility,
    start_rate,
    cash_flows,
    flows_out,
    discount_out,
    done_out,
    reach_ref,
    total_ref,
    part_ref,
    level_ref,
    flow_send,
    flow_recv,
    part_send,
    part_recv,
    level_send,
    level_recv,
    up_send,
    up_recv,
    down_send,
    down_recv,
    side_send,
    side_recv,
    twin_send,
    twin_recv,
    own_sem,
    ready,
):
    rows, width = shocks.shape
    legs = cash_flows.shape[0]
    own = cash_flows.shape[2] // n
    team = sides * CORES
    depth = n // team
    me = lax.axis_index("month")
    z, spot = me // team, me % team
    side, core = spot // CORES, spot % CORES
    place = lambda z, side, core: (z * sides + side) * CORES + core

    def remote(src, dst, send, recv, device):
        return pltpu.make_async_remote_copy(
            src_ref=src,
            dst_ref=dst,
            send_sem=send,
            recv_sem=recv,
            device_id={"month": device},
            device_id_type=MESH,
        )

    barrier = pltpu.get_barrier_semaphore()

    def greet(semaphore, device):
        pl.semaphore_signal(semaphore, inc=1, device_id={"month": device}, device_id_type=MESH)

    for k in range(1, team):
        greet(barrier, z * team + (spot + k) % team)
    for k in range(1, depth):

        @pl.when(z + k < depth)
        def _():
            for j in range(team):
                greet(barrier, (z + k) * team + j)

    def keep(leg):
        return pltpu.make_async_copy(
            cash_flows.at[leg, :, pl.ds(pl.multiple_of(me * own, own), own)],
            flows_out.at[pl.ds(pl.multiple_of(me * rows, rows), rows), pl.ds(leg * own, own)],
            own_sem.at[leg],
        )

    for leg in range(legs):
        keep(leg).start()
    pl.semaphore_wait(barrier, z * team + team - 1)
    for k in range(1, depth):

        @pl.when(z - k >= 0)
        def _():
            for j in range(team):
                greet(ready.at[z], (z - k) * team + j)

    upper = z * 2 // depth
    low_order, high_order = orders(n, team, legs)

    def flow_copy(leg, slot, sender, receiver, device):
        return remote(
            cash_flows.at[leg, :, pl.ds(pl.multiple_of(receiver * own, own), own)],
            flows_out.at[pl.ds(pl.multiple_of(sender * rows, rows), rows), pl.ds(leg * own, own)],
            flow_send.at[slot],
            flow_recv.at[slot],
            device,
        )

    def flow_out(i):
        (leg_a, step_a), (leg_b, step_b) = low_order[i], high_order[i]
        leg = leg_a + upper * (leg_b - leg_a)
        step = step_a + upper * (step_b - step_a)
        to_a, to_b = partners(n, me, step_a)[0], partners(n, me, step_b)[0]
        to = to_a + upper * (to_b - to_a)
        return flow_copy(leg, leg * (n - 1) + step - 1, me, to, to)

    def flow_in(leg, step):
        source = partners(n, me, step)[1]
        return flow_copy(leg, leg * (n - 1) + step - 1, source, me, source)

    count = (n - 1) * legs
    started, sent = [0], [0]

    def fill(upto, window=WINDOW):
        for i in range(started[0], min(count, upto)):
            while i - sent[0] >= window:
                flow_out(sent[0]).wait_send()
                sent[0] += 1
            flow_out(i).start()
            started[0] += 1

    fill(EARLY)

    chunk = math.gcd(width, 256)
    row = lax.broadcasted_iota(jnp.int32, (rows, chunk), 0)
    mean = jnp.zeros((rows, chunk), jnp.float32)
    for t in range(rows):
        mean = jnp.where(row == t, long_mean[t], mean)

    def earlier(x, k):
        if k % 8 == 0:
            return jnp.concatenate([jnp.zeros((k, chunk), jnp.float32), x[: rows - k]], axis=0)
        return jnp.where(row >= k, pltpu.roll(x, k, 0), 0.0)

    last = []
    for c in range(width // chunk):
        lanes = pl.ds(c * chunk, chunk)
        pull = reversion[lanes].reshape(1, chunk) * month_step
        sway = volatility[lanes].reshape(1, chunk) * root_step
        shock = shocks[:, lanes]
        rate = pull * mean + sway * shock
        total = rate + (price_scale * shock + price_drift)
        power = 1.0 - pull
        reach = power
        powers = jnp.broadcast_to(power, (rows, chunk))
        reaches = powers
        k = 1
        while k < rows:
            before = earlier(rate, k)
            total = total + earlier(total, k) + reach * before
            rate = rate + power * before
            later = row // k % 2 == 1
            reaches = jnp.where(later, reaches + powers * reach, reaches)
            powers = jnp.where(later, powers * power, powers)
            reach = reach + power * reach
            power = power * power
            k *= 2
        reach_ref[:, lanes] = reaches
        total_ref[:, lanes] = total
        part_ref[spot, 0:1, lanes] = rate[rows - 1 :]
        part_ref[spot, 1:2, lanes] = total[rows - 1 :]
        last.append((power, reach))
    power = jnp.concatenate([one[0] for one in last], axis=1)
    reach = jnp.concatenate([one[1] for one in last], axis=1)

    def part_copy(k, slot, device):
        return remote(
            part_ref.at[slot], part_ref.at[slot], part_send.at[k], part_recv.at[k], device
        )

    for k in range(1, team):
        part_copy(k, spot, z * team + (spot + k) % team).start()
    for k in range(1, depth):

        @pl.when(z + k < depth)
        def _():
            pl.semaphore_wait(ready.at[z + k], team)

    fill(PARTS)
    for k in range(1, team):
        source = (spot + team - k) % team
        part_copy(k, source, z * team + source).wait_recv()

    rate, total = part_ref[0, 0:1], part_ref[0, 1:2]
    level_power, level_reach = power, reach
    for j in range(1, team):
        rate, total = (
            power * rate + part_ref[j, 0:1],
            total + reach * rate + part_ref[j, 1:2],
        )
        level_reach = level_reach + reach * level_power
        level_power = power * level_power
    def level_copy():
        return remote(
            level_ref.at[1],
            level_ref.at[0],
            level_send.at[0],
            level_recv.at[0],
            place(z + 1, side, core),
        )

    @pl.when(z == 0)
    def _():
        level_ref[0, 0:1] = start_rate[...].reshape(1, width)
        level_ref[0, 1:2] = jnp.zeros((1, width), jnp.float32)

    @pl.when(z > 0)
    def _():
        level_copy().wait_recv()

    state = (level_ref[0, 0:1], level_ref[0, 1:2])

    @pl.when(z + 1 < depth)
    def _():
        level_ref[1, 0:1] = level_power * state[0] + rate
        level_ref[1, 1:2] = state[1] + level_reach * state[0] + total
        level_copy().start()

    fill(LEVELS)

    def past_part(j, state):
        rate, total = state
        return power * rate + part_ref[j, 0:1], total + reach * rate + part_ref[j, 1:2]

    rate, total = lax.fori_loop(0, spot, past_part, state)
    exponent = total + reach_ref[...] * rate + total_ref[...]
    discount_out[pl.ds(pl.multiple_of(me * rows, rows), rows), :] = jnp.exp(
        -month_step * exponent
    ).astype(jnp.bfloat16)

    def months(m, lanes=slice(None)):
        return discount_out.at[pl.ds(pl.multiple_of(m * rows, rows), rows), lanes]

    waits = []

    def send(cond, make, pieces=1):
        waits.append((cond, make))

        def go():
            for k in range(pieces):
                make(pl.ds(k * (width // pieces), width // pieces)).start()

        if cond is None:
            go()
        else:
            pl.when(cond)(go)

    def shard_copy(shard, lanes, send_sem, recv_sem, device):
        ref = months(shard) if lanes is None else months(shard, lanes)
        return remote(ref, ref, send_sem, recv_sem, device)

    def up_copy(h, shard, device, lanes=None):
        return shard_copy(shard, lanes, up_send.at[h], up_recv.at[h], device)

    def down_copy(h, shard, device, lanes=None):
        return shard_copy(shard, lanes, down_send.at[h], down_recv.at[h], device)

    def side_copy(level, shard, device, lanes=None):
        return shard_copy(shard, lanes, side_send.at[level], side_recv.at[level], device)

    def twin_copy(level, lane, shard, device, lanes=None):
        slot = level * sides + lane
        return shard_copy(shard, lanes, twin_send.at[slot], twin_recv.at[slot], device)

    def beside(cond, level):
        shard = place(level, side, core)
        if sides > 1:
            send(
                cond,
                lambda lanes=None: side_copy(level, shard, place(z, 1 - side, core), lanes),
                SIDE_PIECES,
            )
        send(cond, lambda lanes=None: twin_copy(level, side, shard, place(z, side, 1 - core), lanes))

    def across(cond, level):
        shard = place(level, 1 - side, core)

        def take():
            side_copy(level, shard, place(z, 1 - side, core)).wait_recv()

        if cond is None:
            take()
        else:
            pl.when(cond)(take)
        send(
            cond,
            lambda lanes=None: twin_copy(level, 1 - side, shard, place(z, side, 1 - core), lanes),
        )

    def rise(cond, h, shard):
        send(
            cond,
            lambda lanes=None: up_copy(h, shard, place(z + 1, side, core), lanes),
            PIECES,
        )

    def sink(cond, h, shard):
        send(
            cond,
            lambda lanes=None: down_copy(h, shard, place(z - 1, side, core), lanes),
            PIECES,
        )

    rise(z + 1 < depth, 0, me)
    sink(z > 0, 0, me)
    beside(None, z)
    pace = (count - OWN - LAST) // depth
    fill(OWN + pace)
    for h in range(1, depth):
        low, high = place(z - h, side, core), place(z + h, side, core)

        @pl.when(z - h >= 0)
        def _():
            up_copy(h - 1, low, place(z - 1, side, core)).wait_recv()

        rise((z - h >= 0) & (z + 1 < depth), h, low)

        @pl.when(z + h < depth)
        def _():
            down_copy(h - 1, high, place(z + 1, side, core)).wait_recv()

        sink((z + h < depth) & (z > 0), h, high)
        beside(z - h >= 0, z - h)
        beside(z + h < depth, z + h)
        if sides > 1:
            if h == 1:
                across(None, z)
            else:
                across(z - h + 1 >= 0, z - h + 1)
                across(z + h - 1 < depth, z + h - 1)
        fill(OWN + (1 + h) * pace)
    if sides > 1:
        if depth == 1:
            across(None, z)
        else:
            across(z - depth + 1 >= 0, z - depth + 1)
            across(z + depth - 1 < depth, z + depth - 1)
    fill(count, count)

    for level in range(depth):
        for lane in range(sides):
            shard = place(level, lane, 1 - core)
            twin_copy(level, lane, shard, place(z, side, 1 - core)).wait_recv()
    for leg in range(legs):
        for step in range(1, n):
            flow_in(leg, step).wait_recv()
        keep(leg).wait()
        if leg < legs - 1:
            product(flows_out, discount_out, leg * own, own, done_out, leg * own)
    for k in range(1, team):
        part_copy(k, spot, z * team + (spot + k) % team).wait_send()
    @pl.when(z + 1 < depth)
    def _():
        level_copy().wait_send()

    for cond, make in waits:
        if cond is None:
            make().wait_send()
        else:
            pl.when(cond)(lambda make=make: make().wait_send())
    for i in range(sent[0], count):
        flow_out(i).wait_send()


def local(n, sides, shocks, long_mean, reversion, volatility, start_rate, cash_flows):
    rows, width = shocks.shape
    legs, _, cells = cash_flows.shape
    own = cells // n
    team = sides * CORES
    depth = n // team
    count = (n - 1) * legs
    held = 2 * (n * rows * (legs * own + width) + (legs - 1) * own * width) + SLACK
    dma = pltpu.SemaphoreType.DMA
    vmem = pl.BlockSpec(memory_space=pltpu.VMEM)
    anywhere = pl.BlockSpec(memory_space=pltpu.HBM)
    flows, discount, done = pl.pallas_call(
        functools.partial(kernel, n, sides),
        out_shape=(
            pltpu.VMEM((n * rows, legs * own), jnp.bfloat16),
            pltpu.VMEM((n * rows, width), jnp.bfloat16),
            pltpu.VMEM(((legs - 1) * own, width), jnp.bfloat16),
        ),
        in_specs=[vmem, pl.BlockSpec(memory_space=pltpu.SMEM), vmem, vmem, vmem, anywhere],
        out_specs=(vmem, vmem, vmem),
        scratch_shapes=[
            pltpu.VMEM((rows, width), jnp.float32),
            pltpu.VMEM((rows, width), jnp.float32),
            pltpu.VMEM((team, 2, width), jnp.float32),
            pltpu.VMEM((2, 2, width), jnp.float32),
            dma((count,)),
            dma((count,)),
            dma((team,)),
            dma((team,)),
            dma((1,)),
            dma((1,)),
            dma((depth,)),
            dma((depth,)),
            dma((depth,)),
            dma((depth,)),
            dma((depth,)),
            dma((depth,)),
            dma((n // CORES,)),
            dma((n // CORES,)),
            dma((legs,)),
            pltpu.SemaphoreType.REGULAR((depth,)),
        ],
        compiler_params=pltpu.CompilerParams(
            collective_id=0, has_side_effects=True, vmem_limit_bytes=VMEM_BYTES - held
        ),
        name="exchange",
    )(shocks, long_mean, reversion, volatility, start_rate, cash_flows)
    tiles = own // math.gcd(own, 256)
    present = pl.pallas_call(
        finish,
        out_shape=jax.ShapeDtypeStruct((legs * own, width), jnp.bfloat16),
        in_specs=[vmem, vmem, vmem],
        out_specs=anywhere,
        scratch_shapes=[
            pltpu.VMEM((own, width), jnp.bfloat16),
            dma((legs - 1 + tiles,)),
        ],
        compiler_params=pltpu.CompilerParams(vmem_limit_bytes=16 << 20),
        name="finish",
    )(flows, discount, done)
    return present.reshape(legs, own, width)


def solution(mesh):
    n = mesh.shape["month"]
    sides = max(1, 4 // mesh.shape["groups"])
    placed = (
        P("month", "groups"),
        P("month"),
        P("groups"),
        P("groups"),
        P("groups"),
        P(None, "month", "groups"),
    )
    return jax.shard_map(
        functools.partial(local, n, sides),
        mesh=mesh,
        in_specs=placed,
        out_specs=P(None, ("groups", "month"), None),
        check_vma=False,
    )
```

```python
import functools
import math

import jax
import jax.numpy as jnp
from jax import lax
from jax.experimental import pallas as pl
from jax.experimental.pallas import tpu as pltpu
from jax.sharding import PartitionSpec as P

month_step = 1.0 / 12.0
root_step = math.sqrt(1.0 / 12.0)
risk_price = 0.15
price_scale = risk_price * math.sqrt(12.0)
price_drift = 0.5 * risk_price * risk_price
MESH = pl.DeviceIdType.MESH
CORES = 2
VMEM_BYTES = 67_043_328
SLACK = 65536


WINDOW, EARLY, PARTS, LEVELS, OWN, LAST = 8, 4, 10, 12, 14, 4
PIECES, SIDE_PIECES = 1, 1


def partners(n, me, step):
    if n & (n - 1):
        return (me + step) % n, (me + n - step) % n
    other, bit = me, 1
    while bit < n:
        if step & bit:
            other = other + bit * (1 - 2 * (me // bit % 2))
        bit *= 2
    return other, other


def weave(far, near):
    total = len(far) + len(near)
    out, taken = [], 0
    for i in range(total):
        if taken * total < (i + 1) * len(far) and taken < len(far):
            out.append(far[taken])
            taken += 1
        else:
            out.append(near[i - taken])
    return out


def orders(n, team, legs):
    far = [k for k in range(n // 2, n)]
    near = [k for k in range(team, n // 2)]
    home = [k for k in range(1, min(team, n))]
    low = [(leg, k) for k in home for leg in range(legs)]
    low, rest = low[:EARLY], low[EARLY:]
    high = []
    for leg in range(legs):
        close = [(leg, k) for k in near] + [k for k in rest if k[0] == leg]
        low += weave([(leg, k) for k in far], close)
        high += [(leg, k) for k in weave(far, home + near)]
    return low, high


def product(flows, discount, first, cells, out, row, after=None):
    width = discount.shape[1]
    tall, wide = math.gcd(cells, 256), math.gcd(width, 1024)
    for tile in range(cells // tall):
        for c in range(width // wide):
            cols = pl.ds(c * wide, wide)
            value = lax.dot_general(
                flows[:, pl.ds(first + tile * tall, tall)],
                discount[:, cols],
                (((0,), (0,)), ((), ())),
                preferred_element_type=jnp.float32,
            )
            out[pl.ds(row + tile * tall, tall), cols] = value.astype(jnp.bfloat16)
        if after is not None:
            after(tile, tall)


def finish(flows, discount, done, out, last, sems):
    cells = last.shape[0]
    ready, width = done.shape
    parts = ready // cells

    def ship(k):
        rows = pl.ds(k * cells, cells)
        return pltpu.make_async_copy(done.at[rows], out.at[rows], sems.at[k])

    def tail(tile, tall):
        return pltpu.make_async_copy(
            last.at[pl.ds(tile * tall, tall)],
            out.at[pl.ds(ready + tile * tall, tall)],
            sems.at[parts + tile],
        )

    for k in range(parts):
        ship(k).start()
    product(flows, discount, ready, cells, last, 0, lambda tile, tall: tail(tile, tall).start())
    for k in range(parts):
        ship(k).wait()
    tall = math.gcd(cells, 256)
    for tile in range(cells // tall):
        tail(tile, tall).wait()


def kernel(
    n,
    sides,
    shocks,
    long_mean,
    reversion,
    volatility,
    start_rate,
    cash_flows,
    flows_out,
    discount_out,
    done_out,
    reach_ref,
    total_ref,
    part_ref,
    level_ref,
    flow_send,
    flow_recv,
    part_send,
    part_recv,
    level_send,
    level_recv,
    up_send,
    up_recv,
    down_send,
    down_recv,
    side_send,
    side_recv,
    twin_send,
    twin_recv,
    own_sem,
    ready,
):
    rows, width = shocks.shape
    legs = cash_flows.shape[0]
    own = cash_flows.shape[2] // n
    team = sides * CORES
    depth = n // team
    me = lax.axis_index("month")
    z, spot = me // team, me % team
    side, core = spot // CORES, spot % CORES
    place = lambda z, side, core: (z * sides + side) * CORES + core

    def remote(src, dst, send, recv, device):
        return pltpu.make_async_remote_copy(
            src_ref=src,
            dst_ref=dst,
            send_sem=send,
            recv_sem=recv,
            device_id={"month": device},
            device_id_type=MESH,
        )

    barrier = pltpu.get_barrier_semaphore()

    def greet(semaphore, device):
        pl.semaphore_signal(semaphore, inc=1, device_id={"month": device}, device_id_type=MESH)

    for k in range(1, team):
        greet(barrier, z * team + (spot + k) % team)
    for k in range(1, depth):

        @pl.when(z + k < depth)
        def _():
            for j in range(team):
                greet(barrier, (z + k) * team + j)

    def keep(leg):
        return pltpu.make_async_copy(
            cash_flows.at[leg, :, pl.ds(pl.multiple_of(me * own, own), own)],
            flows_out.at[pl.ds(pl.multiple_of(me * rows, rows), rows), pl.ds(leg * own, own)],
            own_sem.at[leg],
        )

    for leg in range(legs):
        keep(leg).start()
    pl.semaphore_wait(barrier, z * team + team - 1)
    for k in range(1, depth):

        @pl.when(z - k >= 0)
        def _():
            for j in range(team):
                greet(ready.at[z], (z - k) * team + j)

    upper = z * 2 // depth
    low_order, high_order = orders(n, team, legs)

    def flow_copy(leg, slot, sender, receiver, device):
        return remote(
            cash_flows.at[leg, :, pl.ds(pl.multiple_of(receiver * own, own), own)],
            flows_out.at[pl.ds(pl.multiple_of(sender * rows, rows), rows), pl.ds(leg * own, own)],
            flow_send.at[slot],
            flow_recv.at[slot],
            device,
        )

    def flow_out(i):
        (leg_a, step_a), (leg_b, step_b) = low_order[i], high_order[i]
        leg = leg_a + upper * (leg_b - leg_a)
        step = step_a + upper * (step_b - step_a)
        to_a, to_b = partners(n, me, step_a)[0], partners(n, me, step_b)[0]
        to = to_a + upper * (to_b - to_a)
        return flow_copy(leg, leg * (n - 1) + step - 1, me, to, to)

    def flow_in(leg, step):
        source = partners(n, me, step)[1]
        return flow_copy(leg, leg * (n - 1) + step - 1, source, me, source)

    count = (n - 1) * legs
    started, sent = [0], [0]

    def fill(upto, window=WINDOW):
        for i in range(started[0], min(count, upto)):
            while i - sent[0] >= window:
                flow_out(sent[0]).wait_send()
                sent[0] += 1
            flow_out(i).start()
            started[0] += 1

    fill(EARLY)

    chunk = math.gcd(width, 256)
    row = lax.broadcasted_iota(jnp.int32, (rows, chunk), 0)
    mean = jnp.zeros((rows, chunk), jnp.float32)
    for t in range(rows):
        mean = jnp.where(row == t, long_mean[t], mean)

    def earlier(x, k):
        if k % 8 == 0:
            return jnp.concatenate([jnp.zeros((k, chunk), jnp.float32), x[: rows - k]], axis=0)
        return jnp.where(row >= k, pltpu.roll(x, k, 0), 0.0)

    last = []
    for c in range(width // chunk):
        lanes = pl.ds(c * chunk, chunk)
        pull = reversion[lanes].reshape(1, chunk) * month_step
        sway = volatility[lanes].reshape(1, chunk) * root_step
        shock = shocks[:, lanes]
        rate = pull * mean + sway * shock
        total = rate + (price_scale * shock + price_drift)
        power = 1.0 - pull
        reach = power
        powers = jnp.broadcast_to(power, (rows, chunk))
        reaches = powers
        k = 1
        while k < rows:
            before = earlier(rate, k)
            total = total + earlier(total, k) + reach * before
            rate = rate + power * before
            later = row // k % 2 == 1
            reaches = jnp.where(later, reaches + powers * reach, reaches)
            powers = jnp.where(later, powers * power, powers)
            reach = reach + power * reach
            power = power * power
            k *= 2
        reach_ref[:, lanes] = reaches
        total_ref[:, lanes] = total
        part_ref[spot, 0:1, lanes] = rate[rows - 1 :]
        part_ref[spot, 1:2, lanes] = total[rows - 1 :]
        last.append((power, reach))
    power = jnp.concatenate([one[0] for one in last], axis=1)
    reach = jnp.concatenate([one[1] for one in last], axis=1)

    def part_copy(k, slot, device):
        return remote(
            part_ref.at[slot], part_ref.at[slot], part_send.at[k], part_recv.at[k], device
        )

    for k in range(1, team):
        part_copy(k, spot, z * team + (spot + k) % team).start()
    for k in range(1, depth):

        @pl.when(z + k < depth)
        def _():
            pl.semaphore_wait(ready.at[z + k], team)

    fill(PARTS)
    for k in range(1, team):
        source = (spot + team - k) % team
        part_copy(k, source, z * team + source).wait_recv()

    rate, total = part_ref[0, 0:1], part_ref[0, 1:2]
    level_power, level_reach = power, reach
    for j in range(1, team):
        rate, total = (
            power * rate + part_ref[j, 0:1],
            total + reach * rate + part_ref[j, 1:2],
        )
        level_reach = level_reach + reach * level_power
        level_power = power * level_power
    def level_copy():
        return remote(
            level_ref.at[1],
            level_ref.at[0],
            level_send.at[0],
            level_recv.at[0],
            place(z + 1, side, core),
        )

    @pl.when(z == 0)
    def _():
        level_ref[0, 0:1] = start_rate[...].reshape(1, width)
        level_ref[0, 1:2] = jnp.zeros((1, width), jnp.float32)

    @pl.when(z > 0)
    def _():
        level_copy().wait_recv()

    state = (level_ref[0, 0:1], level_ref[0, 1:2])

    @pl.when(z + 1 < depth)
    def _():
        level_ref[1, 0:1] = level_power * state[0] + rate
        level_ref[1, 1:2] = state[1] + level_reach * state[0] + total
        level_copy().start()

    fill(LEVELS)

    def past_part(j, state):
        rate, total = state
        return power * rate + part_ref[j, 0:1], total + reach * rate + part_ref[j, 1:2]

    rate, total = lax.fori_loop(0, spot, past_part, state)
    exponent = total + reach_ref[...] * rate + total_ref[...]
    discount_out[pl.ds(pl.multiple_of(me * rows, rows), rows), :] = jnp.exp(
        -month_step * exponent
    ).astype(jnp.bfloat16)

    def months(m, lanes=slice(None)):
        return discount_out.at[pl.ds(pl.multiple_of(m * rows, rows), rows), lanes]

    waits = []

    def send(cond, make, pieces=1):
        waits.append((cond, make))

        def go():
            for k in range(pieces):
                make(pl.ds(k * (width // pieces), width // pieces)).start()

        if cond is None:
            go()
        else:
            pl.when(cond)(go)

    def shard_copy(shard, lanes, send_sem, recv_sem, device):
        ref = months(shard) if lanes is None else months(shard, lanes)
        return remote(ref, ref, send_sem, recv_sem, device)

    def up_copy(h, shard, device, lanes=None):
        return shard_copy(shard, lanes, up_send.at[h], up_recv.at[h], device)

    def down_copy(h, shard, device, lanes=None):
        return shard_copy(shard, lanes, down_send.at[h], down_recv.at[h], device)

    def side_copy(level, shard, device, lanes=None):
        return shard_copy(shard, lanes, side_send.at[level], side_recv.at[level], device)

    def twin_copy(level, lane, shard, device, lanes=None):
        slot = level * sides + lane
        return shard_copy(shard, lanes, twin_send.at[slot], twin_recv.at[slot], device)

    def beside(cond, level):
        shard = place(level, side, core)
        if sides > 1:
            send(
                cond,
                lambda lanes=None: side_copy(level, shard, place(z, 1 - side, core), lanes),
                SIDE_PIECES,
            )
        send(cond, lambda lanes=None: twin_copy(level, side, shard, place(z, side, 1 - core), lanes))

    def across(cond, level):
        shard = place(level, 1 - side, core)

        def take():
            side_copy(level, shard, place(z, 1 - side, core)).wait_recv()

        if cond is None:
            take()
        else:
            pl.when(cond)(take)
        send(
            cond,
            lambda lanes=None: twin_copy(level, 1 - side, shard, place(z, side, 1 - core), lanes),
        )

    def rise(cond, h, shard):
        send(
            cond,
            lambda lanes=None: up_copy(h, shard, place(z + 1, side, core), lanes),
            PIECES,
        )

    def sink(cond, h, shard):
        send(
            cond,
            lambda lanes=None: down_copy(h, shard, place(z - 1, side, core), lanes),
            PIECES,
        )

    rise(z + 1 < depth, 0, me)
    sink(z > 0, 0, me)
    beside(None, z)
    pace = (count - OWN - LAST) // depth
    fill(OWN + pace)
    for h in range(1, depth):
        low, high = place(z - h, side, core), place(z + h, side, core)

        @pl.when(z - h >= 0)
        def _():
            up_copy(h - 1, low, place(z - 1, side, core)).wait_recv()

        rise((z - h >= 0) & (z + 1 < depth), h, low)

        @pl.when(z + h < depth)
        def _():
            down_copy(h - 1, high, place(z + 1, side, core)).wait_recv()

        sink((z + h < depth) & (z > 0), h, high)
        beside(z - h >= 0, z - h)
        beside(z + h < depth, z + h)
        if sides > 1:
            if h == 1:
                across(None, z)
            else:
                across(z - h + 1 >= 0, z - h + 1)
                across(z + h - 1 < depth, z + h - 1)
        fill(OWN + (1 + h) * pace)
    if sides > 1:
        if depth == 1:
            across(None, z)
        else:
            across(z - depth + 1 >= 0, z - depth + 1)
            across(z + depth - 1 < depth, z + depth - 1)
    fill(count, count)

    for level in range(depth):
        for lane in range(sides):
            shard = place(level, lane, 1 - core)
            twin_copy(level, lane, shard, place(z, side, 1 - core)).wait_recv()
    for leg in range(legs):
        for step in range(1, n):
            flow_in(leg, step).wait_recv()
        keep(leg).wait()
        if leg < legs - 1:
            product(flows_out, discount_out, leg * own, own, done_out, leg * own)
    for k in range(1, team):
        part_copy(k, spot, z * team + (spot + k) % team).wait_send()
    @pl.when(z + 1 < depth)
    def _():
        level_copy().wait_send()

    for cond, make in waits:
        if cond is None:
            make().wait_send()
        else:
            pl.when(cond)(lambda make=make: make().wait_send())
    for i in range(sent[0], count):
        flow_out(i).wait_send()


def local(n, sides, shocks, long_mean, reversion, volatility, start_rate, cash_flows):
    rows, width = shocks.shape
    legs, _, cells = cash_flows.shape
    own = cells // n
    team = sides * CORES
    depth = n // team
    count = (n - 1) * legs
    held = 2 * (n * rows * (legs * own + width) + (legs - 1) * own * width) + SLACK
    dma = pltpu.SemaphoreType.DMA
    vmem = pl.BlockSpec(memory_space=pltpu.VMEM)
    anywhere = pl.BlockSpec(memory_space=pltpu.HBM)
    flows, discount, done = pl.pallas_call(
        functools.partial(kernel, n, sides),
        out_shape=(
            pltpu.VMEM((n * rows, legs * own), jnp.bfloat16),
            pltpu.VMEM((n * rows, width), jnp.bfloat16),
            pltpu.VMEM(((legs - 1) * own, width), jnp.bfloat16),
        ),
        in_specs=[vmem, pl.BlockSpec(memory_space=pltpu.SMEM), vmem, vmem, vmem, anywhere],
        out_specs=(vmem, vmem, vmem),
        scratch_shapes=[
            pltpu.VMEM((rows, width), jnp.float32),
            pltpu.VMEM((rows, width), jnp.float32),
            pltpu.VMEM((team, 2, width), jnp.float32),
            pltpu.VMEM((2, 2, width), jnp.float32),
            dma((count,)),
            dma((count,)),
            dma((team,)),
            dma((team,)),
            dma((1,)),
            dma((1,)),
            dma((depth,)),
            dma((depth,)),
            dma((depth,)),
            dma((depth,)),
            dma((depth,)),
            dma((depth,)),
            dma((n // CORES,)),
            dma((n // CORES,)),
            dma((legs,)),
            pltpu.SemaphoreType.REGULAR((depth,)),
        ],
        compiler_params=pltpu.CompilerParams(
            collective_id=0, has_side_effects=True, vmem_limit_bytes=VMEM_BYTES - held
        ),
        name="exchange",
    )(shocks, long_mean, reversion, volatility, start_rate, cash_flows)
    tiles = own // math.gcd(own, 256)
    present = pl.pallas_call(
        finish,
        out_shape=jax.ShapeDtypeStruct((legs * own, width), jnp.bfloat16),
        in_specs=[vmem, vmem, vmem],
        out_specs=anywhere,
        scratch_shapes=[
            pltpu.VMEM((own, width), jnp.bfloat16),
            dma((legs - 1 + tiles,)),
        ],
        compiler_params=pltpu.CompilerParams(vmem_limit_bytes=16 << 20),
        name="finish",
    )(flows, discount, done)
    return present.reshape(legs, own, width)


def solution(mesh):
    n = mesh.shape["month"]
    sides = max(1, 4 // mesh.shape["groups"])
    placed = (
        P("month", "groups"),
        P("month"),
        P("groups"),
        P("groups"),
        P("groups"),
        P(None, "month", "groups"),
    )
    return jax.shard_map(
        functools.partial(local, n, sides),
        mesh=mesh,
        in_specs=placed,
        out_specs=P(None, ("groups", "month"), None),
        check_vma=False,
    )
```
